512 devices in a mesh: dp: 4 (over y), expert: 128 (over z, x, core).
Axes of the slice: x: 4, y: 4, z: 16, core: 2. Of those that a mesh axis runs over, the one named last changes fastest.
Arguments:
- grad_out: bfloat16 [16384, 4096], P(('dp', 'expert')), may hold values from -6 to 6
- expert_ids: int32 [16384, 8], P(('dp', 'expert')), may hold values from 0 to 127, all different within a row; in each aligned block of 32 rows (0 to 31, 32 to 63, ...) at most 2 rows name the same one
- route_weights: float32 [16384, 8], P(('dp', 'expert')), may hold values from 0.02 to 0.2
- hidden_act: bfloat16 [4, 128, 256, 1536], P('dp', 'expert'), may hold values from -6 to 6
- projection: bfloat16 [128, 1536, 256], P('expert', 'dp'), may hold values from -0.15625 to 0.15625
Outputs:
- projected_grad: bfloat16 [128, 4096, 256], P('expert', 'dp')
The draws below stay inside these ranges and needn't reach their ends.
Inputs may be any that keep to these rules, and one draw needn't show every extreme that they name: `expert_ids`: each row names 8 different experts. Among the 32 tokens of one device (aligned blocks of rows), no expert is named more than 2 times, a bound that some block reaches.
All inputs are finite; a program needn't handle non-finite values.
Results may differ from the reference program's by a relative error of at most 0.0058.
Values may be sent and summed in bfloat16 or wider, within the bound.
No kernel may reach another device: no remote copies, remote signals or barrier semaphores. Data moves between devices by JAX's collectives and lax.ppermute only.
A program may use at most 64 MiB of HBM per device.

```python
import math
import jax
import jax.numpy as jnp
import numpy as np
from jax import lax

D = 4096
HID = 1536
TOPK = 8
RANK = 256
TOK_DEV = 32
EXPERTS = 128
CAP = 2
SLOTS = 256
ALL_TOKENS = 16384
N_DP = 4
N_EXPERT = 128


def block_levels(stream_key, shape, cuts, smallest, top_value):
    level, own = 1.0, jax.random.fold_in(stream_key, 6)
    for dim, shards_of in cuts:
        heights = jnp.exp(jax.random.uniform(jax.random.fold_in(own, dim), (shards_of,), jnp.float32, smallest / len(cuts), top_value / len(cuts)))
        level = level * jnp.repeat(heights, shape[dim] // shards_of).reshape([-1 if axis == dim else 1 for axis in range(len(shape))])
    return level


def routed_block(key, own, number, rows, number_of, top, bound, skew):
    order = jax.random.permutation(key, number_of)
    packed, ordinary = load_shares(number_of, rows * top, bound, skew, True), load_shares(number_of, rows * top, bound, skew, False)
    places = jnp.arange(number_of)

    def named(tallies, rotation):
        used = int((tallies > 0).sum())
        fixed = max(1, used // 4)
        moved = fixed + (places - fixed + rotation * (used - fixed)) % max(1, number_of - fixed)
        return jnp.zeros((number_of,), jnp.int32).at[order[jnp.where(places < fixed, places, moved)]].set(jnp.asarray(tallies, jnp.int32))

    tallies = jnp.where(number % 4 == 0, named(packed, number // 4), named(ordinary, number - number // 4 - 1))
    mixed = jax.random.permutation(jax.random.fold_in(own, 3), number_of)
    giver, sink = mixed[0:number_of // 2 * 2:2], mixed[1:number_of // 2 * 2:2]
    slack = jnp.minimum(tallies[giver] - 1, bound - tallies[sink]) // 2
    slack = jnp.where((giver == order[0]) | (sink == order[0]) | (tallies[sink] == 0), 0, jnp.maximum(slack, 0))
    moved = jax.random.randint(jax.random.fold_in(own, 4), (number_of // 2,), 0, 1 << 20) % (slack + 1)
    tallies = tallies.at[giver].add(-moved).at[sink].add(moved)
    items = jnp.searchsorted(jnp.cumsum(tallies), jnp.arange(rows * top), side="right").astype(jnp.int32)
    listing = items.reshape(top, rows).T
    listing = listing[jax.random.permutation(jax.random.fold_in(own, 1), rows)]
    rotation = jax.random.randint(jax.random.fold_in(own, 2), (rows, 1), 0, top)
    return jnp.take_along_axis(listing, (jnp.arange(top)[None, :] + rotation) % top, axis=1)


def load_shares(count, total, bound, skew, full):
    portions = [(1 << 20) // math.isqrt(rank ** skew) + 1 for rank in range(1, count + 1)]
    largest = bound if full else min(bound, max(-(-total // count), total * portions[0] // sum(portions)))
    least = 1 if total - largest >= count - 1 else 0
    given, spare = [largest] + [least] * (count - 1), total - largest - least * (count - 1)
    while spare > 0:
        free = [i for i in range(1, count) if given[i] < largest] or [i for i in range(1, count) if given[i] < bound]
        pool, remaining = sum([portions[i] for i in free]), spare
        for i in free:
            more = min(bound - given[i], max(1, remaining * portions[i] // pool), spare)
            given[i] = given[i] + more
            spare = spare - more
    return np.array(given)


def gaussian(key, extent, scale, limit, cuts=(), kind=jnp.bfloat16):
    drawn = scale * jax.random.normal(key, extent, jnp.float32)
    if cuts:
        drawn = drawn * block_levels(key, extent, cuts, -0.22, 0.18)
    return jnp.clip(drawn, -limit, limit).astype(kind)


def setup_inputs(seed: int = 0) -> dict:
    arg_keys = jax.random.split(jax.random.key(seed), 6)
    grad_out = gaussian(arg_keys[0], (ALL_TOKENS, D), 1.0, 6.0, ((0, 512),))
    expert_ids_keys = jax.random.split(jax.random.fold_in(arg_keys[1], 1), ALL_TOKENS // TOK_DEV)
    expert_ids_turns = jax.random.permutation(jax.random.fold_in(arg_keys[1], 3), ALL_TOKENS // TOK_DEV)
    expert_ids = jax.vmap(lambda own, number: routed_block(jax.random.fold_in(arg_keys[1], 2), own, number, TOK_DEV, EXPERTS, TOPK, CAP, 2))(expert_ids_keys, expert_ids_turns).reshape((ALL_TOKENS, TOPK))
    route_weights = jnp.clip(0.02 + 0.18 * jax.random.uniform(arg_keys[2], (ALL_TOKENS, TOPK), jnp.float32) ** block_levels(arg_keys[2], (ALL_TOKENS, TOPK), ((0, 512),), -0.2, 0.2), 0.02, 0.2)
    hidden_act = gaussian(arg_keys[3], (N_DP, EXPERTS, SLOTS, HID), 1.0, 6.0, ((0, 4), (1, 128)))
    projection = gaussian(arg_keys[4], (EXPERTS, HID, RANK), HID ** -0.5, 0.15625, ((0, 128), (1, 4)))
    return {"grad_out": grad_out, "expert_ids": expert_ids, "route_weights": route_weights, "hidden_act": hidden_act, "projection": projection}


def reference(grad_out, expert_ids, route_weights, hidden_act, projection):
    sources = N_DP * N_EXPERT
    per_source = TOK_DEV * TOPK
    routed = expert_ids.reshape(sources, per_source)
    onehot = (routed[:, :, None] == jnp.arange(EXPERTS, dtype=jnp.int32)[None, None, :]).astype(jnp.int32)
    earlier = jnp.cumsum(onehot, axis=1) - onehot
    position = jnp.sum(earlier * onehot, axis=2).astype(jnp.int32)
    slot = (routed * CAP + position).astype(jnp.int32)
    table = jnp.full((sources, EXPERTS * CAP), -1, jnp.int32)
    source_rows = jnp.broadcast_to(jnp.arange(sources, dtype=jnp.int32)[:, None], (sources, per_source))
    route_local = jnp.broadcast_to(jnp.arange(per_source, dtype=jnp.int32)[None, :], (sources, per_source))
    table = table.at[source_rows, slot].set(route_local)
    table = table.reshape(N_DP, N_EXPERT, EXPERTS, CAP)
    flat_weights = route_weights.reshape(-1)

    def one_expert(expert):
        total = jnp.zeros((D, RANK), jnp.float32)
        basis = lax.dynamic_index_in_dim(projection, expert, 0, keepdims=False)
        for replica in range(N_DP):
            picks = lax.dynamic_index_in_dim(table[replica], expert, 1, keepdims=False)
            source_base = ((replica * N_EXPERT + jnp.arange(N_EXPERT, dtype=jnp.int32)) * per_source)[:, None]
            valid = (picks >= 0).reshape(-1)
            route = (source_base + jnp.maximum(picks, 0)).reshape(-1).astype(jnp.int32)
            rows = grad_out[route // TOPK].astype(jnp.float32)
            weight = flat_weights[route]
            weighted = jnp.where(valid[:, None], weight[:, None] * rows, 0.0).astype(jnp.bfloat16)
            hidden = lax.dynamic_index_in_dim(hidden_act[replica], expert, 0, keepdims=False)
            reduced = jnp.dot(hidden, basis, preferred_element_type=jnp.float32).astype(jnp.bfloat16)
            total = total + jnp.dot(weighted.T, reduced, preferred_element_type=jnp.float32)
        return total.astype(jnp.bfloat16)

    return lax.map(one_expert, jnp.arange(EXPERTS, dtype=jnp.int32))
```

```python
import jax
import jax.numpy as jnp
from jax import lax
from jax.experimental import pallas as pl
from jax.experimental.pallas import tpu as pltpu
from jax.sharding import PartitionSpec as P


def weigh_kernel(grad_ref, ids_ref, weight_ref, out_ref):
    tokens = grad_ref.shape[0]
    top_count = ids_ref.shape[0]
    parts, slots, width = out_ref.shape
    row = lax.broadcasted_iota(jnp.int32, (slots, tokens), 0)
    expert = row // 2
    hit = jnp.zeros((slots, tokens), jnp.float32)
    scale = jnp.zeros((slots, tokens), jnp.float32)
    for k in range(top_count):
        same = ids_ref[k : k + 1, :] == expert
        hit = jnp.where(same, 1.0, hit)
        scale = jnp.where(same, weight_ref[k : k + 1, :], scale)
    before = lax.broadcasted_iota(jnp.int32, (tokens, tokens), 0) < lax.broadcasted_iota(
        jnp.int32, (tokens, tokens), 1
    )
    rank = jnp.dot(
        hit.astype(jnp.bfloat16),
        before.astype(jnp.float32).astype(jnp.bfloat16),
        preferred_element_type=jnp.float32,
    )
    wanted = (row % 2).astype(jnp.float32)
    chosen = jnp.where((hit > 0.5) & (jnp.abs(rank - wanted) < 0.5), 1.0, 0.0)
    weight = jnp.sum(chosen * scale, axis=1, keepdims=True)
    chosen = chosen.astype(jnp.bfloat16)
    for part in range(parts):
        rows = jnp.dot(
            chosen, grad_ref[:, part * width : (part + 1) * width], preferred_element_type=jnp.float32
        )
        out_ref[part] = (weight * rows).astype(jnp.bfloat16)


def shards(grad_out, expert_ids, route_weights, hidden_act, projection):
    replicas = lax.axis_size("dp")
    expert_count = lax.axis_size("expert")
    width = grad_out.shape[1] // replicas
    slot_count = hidden_act.shape[2]
    capacity = slot_count // expert_count
    weighted = pl.pallas_call(
        weigh_kernel,
        out_shape=jax.ShapeDtypeStruct((replicas, slot_count, width), jnp.bfloat16),
    )(grad_out, expert_ids.T, route_weights.T)
    outgoing = weighted.reshape(replicas * expert_count, capacity, width)
    arrived = lax.all_to_all(
        outgoing, ("dp", "expert"), split_axis=0, concat_axis=0, tiled=True
    ).reshape(replicas * slot_count, width)
    reduced = jnp.dot(
        hidden_act[0, 0],
        lax.all_gather(projection[0], "dp", axis=0, tiled=True),
        preferred_element_type=jnp.float32,
    ).astype(jnp.bfloat16)
    reduced = lax.all_gather(reduced, "dp", axis=0, tiled=True)
    share = lax.dot_general(
        arrived, reduced, (((0,), (0,)), ((), ())), preferred_element_type=jnp.float32
    )
    return share.astype(jnp.bfloat16)[None]


def solution(mesh):
    in_specs = (
        P(("dp", "expert"), None),
        P(("dp", "expert"), None),
        P(("dp", "expert"), None),
        P("dp", "expert", None, None),
        P("expert", "dp", None),
    )
    out_specs = P("expert", "dp", None)
    return jax.shard_map(shards, mesh=mesh, in_specs=in_specs, out_specs=out_specs, check_vma=False)
```

```python
import numpy as np

import jax
import jax.numpy as jnp
from jax import lax
from jax.experimental import pallas as pl
from jax.experimental.pallas import tpu as pltpu
from jax.sharding import Mesh, PartitionSpec as P


PLANES = 16
LEAP = 4
META = 128
GROUP = 16
F32, BF16 = jnp.float32, jnp.bfloat16

STAY = (0, (0, 1, 2))
UP1, DOWN1 = (1, (0, 1, 2)), (-1, (0, 1, 2))
UP2, DOWN2 = (2, (0, 1)), (-2, (0, 2))
UP3, DOWN3 = (3, (1,)), (-3, (2,))
UP4 = (4, (1,))
MESSAGES = (STAY, UP1, DOWN1, UP2, DOWN2, UP3, DOWN3, UP4)
SMALL = pltpu.CompilerParams(vmem_limit_bytes=12 * 1024 * 1024)
START = (0, -LEAP, LEAP)


def origin(step, block):
    return START[block] - step


ORDER = [origin(step, block) for step, blocks in MESSAGES for block in blocks]


def pack_kernel(grad_ref, ids_ref, weight_ref, out_ref):
    tokens, width = grad_ref.shape
    high = weight_ref[...].astype(BF16).astype(F32)
    rest = weight_ref[...] - high
    middle = rest.astype(BF16).astype(F32)
    low = rest - middle
    parts = [ids_ref[...].astype(F32), high, middle, low]
    used = sum(part.shape[0] for part in parts)
    meta = jnp.concatenate(parts + [jnp.zeros((META - used, tokens), F32)], axis=0)
    same = lax.broadcasted_iota(jnp.int32, (tokens, tokens), 0) == lax.broadcasted_iota(
        jnp.int32, (tokens, tokens), 1
    )
    turned = lax.dot_general(
        same.astype(F32).astype(BF16),
        meta.astype(BF16),
        (((1,), (1,)), ((), ())),
        preferred_element_type=F32,
    )
    out_ref[:, :width] = grad_ref[...]
    out_ref[:, width:] = turned.astype(BF16)


def pick_kernel(place_ref, own_ref, behind_ref, ahead_ref, *out_refs):
    tokens = own_ref.shape[0]
    width = own_ref.shape[1] - META
    top_count = 8
    plane, sign = place_ref[0], place_ref[1]
    square = (META, META)
    same = lax.broadcasted_iota(jnp.int32, square, 0) == lax.broadcasted_iota(jnp.int32, square, 1)
    same = same.astype(F32).astype(BF16)
    before = lax.broadcasted_iota(jnp.int32, (tokens, tokens), 0) < lax.broadcasted_iota(
        jnp.int32, (tokens, tokens), 1
    )
    before = before.astype(F32).astype(BF16)
    row = lax.broadcasted_iota(jnp.int32, (GROUP, tokens), 0)
    for block, ref in enumerate((own_ref, behind_ref, ahead_ref)):
        meta = lax.dot_general(
            same, ref[:, width:], (((1,), (1,)), ((), ())), preferred_element_type=F32
        )
        ids = meta[:top_count].astype(jnp.int32)
        weights = (
            meta[top_count : 2 * top_count] + meta[2 * top_count : 3 * top_count]
        ) + meta[3 * top_count : 4 * top_count]
        places, hits, scales = [], [], []
        for (step, blocks), out_ref in zip(MESSAGES, out_refs, strict=True):
            if block not in blocks:
                continue
            places.append((out_ref, blocks.index(block) * GROUP))
            goal = lax.rem(plane + sign * step + PLANES, PLANES)
            expert = goal * (GROUP // 2) + row // 2
            hit = jnp.zeros((GROUP, tokens), F32)
            scale = jnp.zeros((GROUP, tokens), F32)
            for k in range(top_count):
                found = ids[k : k + 1, :] == expert
                hit = jnp.where(found, 1.0, hit)
                scale = jnp.where(found, weights[k : k + 1, :], scale)
            hits.append(hit)
            scales.append(scale)
        hit, scale = jnp.concatenate(hits, axis=0), jnp.concatenate(scales, axis=0)
        rank = jnp.dot(hit.astype(BF16), before, preferred_element_type=F32)
        wanted = (lax.broadcasted_iota(jnp.int32, hit.shape, 0) % 2).astype(F32)
        chosen = jnp.where((hit > 0.5) & (jnp.abs(rank - wanted) < 0.5), 1.0, 0.0)
        weight = jnp.sum(chosen * scale, axis=1, keepdims=True)
        chosen = chosen.astype(BF16)
        chunk = 1024
        for start in range(0, width, chunk):
            rows = jnp.dot(chosen, ref[:, start : start + chunk], preferred_element_type=F32)
            rows = (weight * rows).astype(BF16)
            for i, (out_ref, at) in enumerate(places):
                out_ref[at : at + GROUP, start : start + chunk] = rows[i * GROUP : (i + 1) * GROUP]


def join_kernel(spans, *refs):
    *in_refs, out_ref = refs
    parts, count, width = out_ref.shape
    blocks = count // GROUP
    shape = (count, count)
    to = lax.broadcasted_iota(jnp.int32, shape, 0)
    at = lax.broadcasted_iota(jnp.int32, shape, 1)
    device, rest = to // (2 * blocks), to % (2 * blocks)
    move = (at == (rest // 2) * GROUP + device * 2 + rest % 2).astype(F32).astype(BF16)
    for part in range(parts):
        cut = pl.ds(part * width, width)
        rows = jnp.concatenate(
            [ref[low:high, cut] for ref, (low, high) in zip(in_refs, spans, strict=True)], axis=0
        )
        out_ref[part] = jnp.dot(move, rows, preferred_element_type=F32).astype(BF16)


def join(pieces, parts):
    spans = tuple((low, high) for _, low, high in pieces)
    rows = sum(high - low for low, high in spans)
    width = pieces[0][0].shape[1] // parts

    def kernel(*refs):
        join_kernel(spans, *refs)

    return pl.pallas_call(
        kernel,
        out_shape=jax.ShapeDtypeStruct((parts, rows, width), BF16),
        compiler_params=SMALL,
    )(*[array for array, _, _ in pieces])


def shift(array, step):
    pairs = []
    for z in range(PLANES):
        for core in range(2):
            goal = (z + (step if core == 0 else -step)) % PLANES
            pairs.append((z * 2 + core, goal * 2 + core))
    return lax.ppermute(array, ("z", "core"), pairs)


def gathered(array, axis):
    count = lax.axis_size(axis)
    copies = jnp.broadcast_to(array[None], (count, *array.shape))
    return lax.all_to_all(copies, axis, split_axis=0, concat_axis=0, tiled=True)


def picked(plane, sign, own, behind, ahead):
    width = own.shape[1] - META
    return pl.pallas_call(
        pick_kernel,
        in_specs=[pl.BlockSpec(memory_space=pltpu.SMEM)] + [pl.BlockSpec(memory_space=pltpu.VMEM)] * 3,
        out_shape=[
            jax.ShapeDtypeStruct((len(blocks) * GROUP, width), BF16) for _, blocks in MESSAGES
        ],
        compiler_params=SMALL,
    )(jnp.stack([plane, sign]).astype(jnp.int32), own, behind, ahead)


def layer(grad_out, expert_ids, route_weights, hidden_act, projection):
    parts = lax.axis_size("dp")
    tokens, width = grad_out.shape
    plane, core = lax.axis_index("z"), lax.axis_index("core")
    sign = 1 - 2 * core
    own = pl.pallas_call(
        pack_kernel,
        out_shape=jax.ShapeDtypeStruct((tokens, width + META), BF16),
        compiler_params=SMALL,
    )(grad_out, expert_ids.T, route_weights.T)
    behind, ahead = shift(own, LEAP), shift(own, -LEAP)

    basis = gathered(projection[0], "dp").reshape(-1, projection.shape[2])
    reduced = jnp.dot(hidden_act[0, 0], basis, preferred_element_type=F32).astype(BF16)
    slots = reduced.shape[0]
    to = jnp.arange(slots, dtype=jnp.int32)
    batch, seat, block, copy = to // 128, (to // 16) % 8, (to // 2) % 8, to % 2
    offset = jnp.asarray(np.array(ORDER, np.int32))
    offset = jnp.sum(
        jnp.where((batch * 8 + block)[:, None] == jnp.arange(PLANES)[None, :], offset[None, :], 0),
        axis=1,
    )
    source = (plane + (1 - 2 * (seat % 2)) * offset) % PLANES
    slot = source * 16 + seat * 2 + copy
    move = (slot[:, None] == jnp.arange(slots, dtype=jnp.int32)[None, :]).astype(BF16)
    reduced = jnp.dot(move, reduced, preferred_element_type=F32).astype(BF16)
    reduced = gathered(reduced, "dp")

    sent = picked(plane, sign, own, behind, ahead)
    came = [
        array if step == 0 else shift(array, step)
        for array, (step, _) in zip(sent, MESSAGES, strict=True)
    ]
    stay, up1, down1, up2, down2, up3, down3, up4 = came
    two = 2 * GROUP
    first = join([(stay, 0, 3 * GROUP), (up1, 0, 3 * GROUP), (down1, 0, two)], parts)
    first, up2 = lax.optimization_barrier((first, up2))
    second = join(
        [
            (down1, two, 3 * GROUP),
            (up2, 0, two),
            (down2, 0, two),
            (up3, 0, GROUP),
            (down3, 0, GROUP),
            (up4, 0, GROUP),
        ],
        parts,
    )
    total = None
    for i, batch in enumerate((first, second)):
        arrived = lax.all_to_all(
            batch.reshape(-1, GROUP, batch.shape[2]),
            ("dp", "x", "core"),
            split_axis=0,
            concat_axis=0,
            tiled=True,
        ).reshape(-1, batch.shape[2])
        half = slots // 2
        factor = reduced[:, i * half : (i + 1) * half].reshape(-1, reduced.shape[2])
        share = lax.dot_general(
            arrived, factor, (((0,), (0,)), ((), ())), preferred_element_type=F32
        )
        total = share if total is None else total + share
    return total.astype(BF16)[None]


def solution(mesh):
    names = ("dp", "z", "x", "core")
    fine = Mesh(mesh.devices.reshape(mesh.shape["dp"], PLANES, -1, 2), names)
    devices = ("z", "x", "core")
    in_specs = (
        P(names, None),
        P(names, None),
        P(names, None),
        P("dp", devices, None, None),
        P(devices, "dp", None),
    )
    out_specs = P(devices, "dp", None)
    return jax.shard_map(layer, mesh=fine, in_specs=in_specs, out_specs=out_specs, check_vma=False)
```

```python
import numpy as np

import jax
import jax.numpy as jnp
from jax import lax
from jax.experimental import pallas as pl
from jax.experimental.pallas import tpu as pltpu
from jax.sharding import Mesh, PartitionSpec as P


PLANES = 16
SEATS = 8
LEAP = 5
META = 128
TOPK = 8
GROUP = 2 * SEATS
F32, BF16 = jnp.float32, jnp.bfloat16
SMALL = pltpu.CompilerParams(vmem_limit_bytes=12 * 1024 * 1024)

START = (0, -LEAP, LEAP)
NEAR = ((1, 0), (1, 1), (1, 2), (0, 0), (-1, 0), (-1, 1), (-1, 2), (0, 1))
FAR = ((0, 2), (2, 0), (2, 1), (2, 2), (-2, 0), (-2, 1), (-2, 2), (3, 1))
CUTS = (GROUP, 3 * GROUP, 3 * GROUP, GROUP)


def origins(table, moved):
    return [(START[block], step) if step == moved else None for step, block in table]


SLOTS = (
    origins(NEAR, 0)
    + origins(NEAR[:4], 1)
    + origins(NEAR[4:], -1)
    + [(START[block] - step, 0) for step, block in FAR]
)


def pack_kernel(grad_ref, ids_ref, weight_ref, out_ref):
    tokens, width = grad_ref.shape
    high = weight_ref[...].astype(BF16).astype(F32)
    rest = weight_ref[...] - high
    middle = rest.astype(BF16).astype(F32)
    low = rest - middle
    parts = [ids_ref[...].astype(F32), high, middle, low]
    used = sum(part.shape[0] for part in parts)
    meta = jnp.concatenate(parts + [jnp.zeros((META - used, tokens), F32)], axis=0)
    same = lax.broadcasted_iota(jnp.int32, (tokens, tokens), 0) == lax.broadcasted_iota(
        jnp.int32, (tokens, tokens), 1
    )
    turned = lax.dot_general(
        same.astype(F32).astype(BF16),
        meta.astype(BF16),
        (((1,), (1,)), ((), ())),
        preferred_element_type=F32,
    )
    out_ref[:, :width] = grad_ref[...]
    out_ref[:, width:] = turned.astype(BF16)


def pick_kernel(place_ref, own_ref, behind_ref, ahead_ref, near_ref, *far_refs):
    refs = (own_ref, behind_ref, ahead_ref)
    tokens = own_ref.shape[0]
    width = own_ref.shape[1] - META
    lanes = tokens * len(refs)
    parts, count, part_width = near_ref.shape
    plane, sign = place_ref[0], place_ref[1]

    same = lax.broadcasted_iota(jnp.int32, (META, META), 0) == lax.broadcasted_iota(
        jnp.int32, (META, META), 1
    )
    meta = lax.dot_general(
        same.astype(F32).astype(BF16),
        jnp.concatenate([ref[:, width:] for ref in refs], axis=0),
        (((1,), (1,)), ((), ())),
        preferred_element_type=F32,
    )
    ids = meta[:TOPK]
    weights = (meta[TOPK : 2 * TOPK] + meta[2 * TOPK : 3 * TOPK]) + meta[3 * TOPK : 4 * TOPK]
    early = lax.broadcasted_iota(jnp.int32, (lanes, lanes), 0)
    late = lax.broadcasted_iota(jnp.int32, (lanes, lanes), 1)
    before = ((early // tokens == late // tokens) & (early < late)).astype(F32).astype(BF16)

    row = lax.broadcasted_iota(jnp.int32, (count, lanes), 0)
    block = lax.broadcasted_iota(jnp.int32, (count, lanes), 1) // tokens
    copy = (row % 2).astype(F32)

    def choose(table, entry, seat, senses):
        base = jnp.zeros((count, lanes), jnp.int32)
        wanted = jnp.zeros((count, lanes), jnp.int32)
        for i, (step, source) in enumerate(table):
            goals = [lax.rem(plane + sense * step + PLANES, PLANES) * SEATS for sense in senses]
            goal = goals[0] if len(goals) == 1 else jnp.where(seat % 2 == 0, goals[0], goals[1])
            base = jnp.where(entry == i, goal, base)
            wanted = jnp.where(entry == i, source, wanted)
        expert = (base + seat).astype(F32)
        hit = jnp.zeros((count, lanes), F32)
        scale = jnp.zeros((count, lanes), F32)
        for k in range(TOPK):
            found = ids[k : k + 1, :] == expert
            hit = jnp.where(found, 1.0, hit)
            scale = jnp.where(found, weights[k : k + 1, :], scale)
        rank = jnp.dot(hit.astype(BF16), before, preferred_element_type=F32)
        chosen = (hit > 0.5) & (jnp.abs(rank - copy) < 0.5) & (block == wanted)
        chosen = jnp.where(chosen, 1.0, 0.0)
        return chosen.astype(BF16), jnp.sum(chosen * scale, axis=1, keepdims=True)

    near, near_weight = choose(NEAR, (row // 2) % 8, row // GROUP, (1, -1))
    far, far_weight = choose(FAR, row // GROUP, (row // 2) % SEATS, (sign,))
    for part in range(parts):
        cut = pl.ds(part * part_width, part_width)
        tile = jnp.concatenate([ref[:, cut] for ref in refs], axis=0)
        rows = jnp.dot(far, tile, preferred_element_type=F32)
        rows = (far_weight * rows).astype(BF16)
        at = 0
        for ref, size in zip(far_refs, CUTS, strict=True):
            ref[:, cut] = rows[at : at + size]
            at += size
        rows = jnp.dot(near, tile, preferred_element_type=F32)
        near_ref[part] = (near_weight * rows).astype(BF16)


def picked(plane, sign, own, behind, ahead, parts):
    width = own.shape[1] - META
    shapes = [(parts, SEATS * GROUP, width // parts)] + [(size, width) for size in CUTS]
    return pl.pallas_call(
        pick_kernel,
        in_specs=[pl.BlockSpec(memory_space=pltpu.SMEM)] + [pl.BlockSpec(memory_space=pltpu.VMEM)] * 3,
        out_shape=[jax.ShapeDtypeStruct(shape, BF16) for shape in shapes],
        compiler_params=SMALL,
    )(jnp.stack([plane, sign]).astype(jnp.int32), own, behind, ahead)


def join_kernel(*refs):
    *in_refs, out_ref = refs
    parts, count, width = out_ref.shape
    to = lax.broadcasted_iota(jnp.int32, (count, count), 0)
    at = lax.broadcasted_iota(jnp.int32, (count, count), 1)
    seat, entry, copy = to // GROUP, (to // 2) % 8, to % 2
    move = (at == entry * GROUP + seat * 2 + copy).astype(F32).astype(BF16)
    for part in range(parts):
        cut = pl.ds(part * width, width)
        rows = jnp.concatenate([ref[:, cut] for ref in in_refs], axis=0)
        out_ref[part] = jnp.dot(move, rows, preferred_element_type=F32).astype(BF16)


def join(pieces, parts):
    rows = sum(piece.shape[0] for piece in pieces)
    return pl.pallas_call(
        join_kernel,
        out_shape=jax.ShapeDtypeStruct((parts, rows, pieces[0].shape[1] // parts), BF16),
        compiler_params=SMALL,
    )(*pieces)


def shift(array, step):
    pairs = []
    for z in range(PLANES):
        for core in range(2):
            goal = (z + (step if core == 0 else -step)) % PLANES
            pairs.append((z * 2 + core, goal * 2 + core))
    return lax.ppermute(array, ("z", "core"), pairs)


def gathered(array, axis):
    count = lax.axis_size(axis)
    copies = jnp.broadcast_to(array[None], (count, *array.shape))
    return lax.all_to_all(copies, axis, split_axis=0, concat_axis=0, tiled=True)


def exchanged(array):
    array = array.reshape(-1, GROUP, array.shape[2])
    return lax.all_to_all(array, ("dp", "x", "core"), split_axis=0, concat_axis=0, tiled=True)


def factor_moves(plane, sign, slots):
    moves = []
    for low, high in ((0, 8), (8, 12), (12, 16), (16, 24)):
        span = SLOTS[low:high]
        size = len(span)
        to = np.arange(SEATS * size * 2)
        seat, entry, copy = to // (size * 2), (to // 2) % size, to % 2
        ahead = np.array([0 if s is None else s[0] for s in span])[entry] * (1 - 2 * (seat % 2))
        behind = np.array([0 if s is None else s[1] for s in span])[entry]
        real = np.array([s is not None for s in span])[entry]
        moves.append(np.stack([ahead, behind, seat * 2 + copy, real]))
    ahead, behind, within, real = np.concatenate(moves, axis=1).astype(np.int32)
    slot = (plane + ahead - sign * behind + 2 * PLANES) % PLANES * GROUP + within
    same = slot[:, None] == jnp.arange(slots, dtype=jnp.int32)[None, :]
    return (same & (real[:, None] > 0)).astype(BF16)


def layer(grad_out, expert_ids, route_weights, hidden_act, projection):
    parts = lax.axis_size("dp")
    tokens, width = grad_out.shape
    rank = projection.shape[2]
    plane, core = lax.axis_index("z"), lax.axis_index("core")
    sign = 1 - 2 * core
    own = pl.pallas_call(
        pack_kernel,
        out_shape=jax.ShapeDtypeStruct((tokens, width + META), BF16),
    )(grad_out, expert_ids.T, route_weights.T)
    behind, ahead = shift(own, LEAP), shift(own, -LEAP)

    basis = gathered(projection[0], "dp").reshape(-1, rank)
    reduced = jnp.dot(hidden_act[0, 0], basis, preferred_element_type=F32).astype(BF16)
    reduced = gathered(reduced, "dp")
    moves = factor_moves(plane, sign, reduced.shape[1])
    factor = jnp.einsum("as,rsk->rak", moves, reduced, preferred_element_type=F32).astype(BF16)

    near, stay, up2, down2, up3 = picked(plane, sign, own, behind, ahead, parts)
    up2, down2, up3 = shift(up2, 2), shift(down2, -2), shift(up3, 3)
    near = exchanged(near)
    far = join([stay, up2, down2, up3], parts)
    far = exchanged(far)
    up1 = shift(near[:, :8], 1)
    down1 = shift(near[:, 8:], -1)
    total = None
    at = 0
    for piece in (near, up1, down1, far):
        size = SEATS * piece.shape[1]
        share = lax.dot_general(
            piece.reshape(-1, piece.shape[2]),
            factor[:, at : at + size].reshape(-1, rank),
            (((0,), (0,)), ((), ())),
            preferred_element_type=F32,
        )
        total = share if total is None else total + share
        at += size
    return total.astype(BF16)[None]


def solution(mesh):
    names = ("dp", "z", "x", "core")
    fine = Mesh(mesh.devices.reshape(mesh.shape["dp"], PLANES, -1, 2), names)
    devices = ("z", "x", "core")
    in_specs = (
        P(names, None),
        P(names, None),
        P(names, None),
        P("dp", devices, None, None),
        P(devices, "dp", None),
    )
    out_specs = P(devices, "dp", None)
    return jax.shard_map(layer, mesh=fine, in_specs=in_specs, out_specs=out_specs, check_vma=False)
```

```python
import numpy as np

import jax
import jax.numpy as jnp
from jax import lax
from jax.experimental import pallas as pl
from jax.experimental.pallas import tpu as pltpu
from jax.sharding import Mesh, PartitionSpec as P


PLANES = 16
SEATS = 8
LEAP = 5
META = 128
TOPK = 8
GROUP = 2 * SEATS
F32, BF16 = jnp.float32, jnp.bfloat16
SMALL = pltpu.CompilerParams(vmem_limit_bytes=12 * 1024 * 1024)

START = (0, -LEAP, LEAP)
NEAR = ((1, 0), (1, 1), (1, 2), (0, 0), (-1, 0), (-1, 1), (-1, 2), (0, 1))
FAR = ((0, 2), (2, 0), (2, 1), (2, 2), (-2, 0), (-2, 1), (-2, 2), (3, 1))
CUTS = (GROUP, 3 * GROUP, 3 * GROUP, GROUP)


def origins(table, moved):
    return [(START[block], step) if step == moved else None for step, block in table]


SLOTS = (
    origins(NEAR, 0)
    + origins(NEAR[:4], 1)
    + origins(NEAR[4:], -1)
    + [(START[block] - step, 0) for step, block in FAR]
)


def pack_kernel(grad_ref, ids_ref, weight_ref, out_ref):
    tokens, width = grad_ref.shape
    high = weight_ref[...].astype(BF16).astype(F32)
    rest = weight_ref[...] - high
    middle = rest.astype(BF16).astype(F32)
    low = rest - middle
    parts = [ids_ref[...].astype(F32), high, middle, low]
    used = sum(part.shape[0] for part in parts)
    meta = jnp.concatenate(parts + [jnp.zeros((META - used, tokens), F32)], axis=0)
    same = lax.broadcasted_iota(jnp.int32, (tokens, tokens), 0) == lax.broadcasted_iota(
        jnp.int32, (tokens, tokens), 1
    )
    turned = lax.dot_general(
        same.astype(F32).astype(BF16),
        meta.astype(BF16),
        (((1,), (1,)), ((), ())),
        preferred_element_type=F32,
    )
    out_ref[:, :width] = grad_ref[...]
    out_ref[:, width:] = turned.astype(BF16)


def pick_kernel(place_ref, own_ref, behind_ref, ahead_ref, near_ref, *far_refs):
    refs = (own_ref, behind_ref, ahead_ref)
    tokens = own_ref.shape[0]
    width = own_ref.shape[1] - META
    lanes = tokens * len(refs)
    parts, count, part_width = near_ref.shape
    plane, sign = place_ref[0], place_ref[1]

    same = lax.broadcasted_iota(jnp.int32, (META, META), 0) == lax.broadcasted_iota(
        jnp.int32, (META, META), 1
    )
    meta = lax.dot_general(
        same.astype(F32).astype(BF16),
        jnp.concatenate([ref[:, width:] for ref in refs], axis=0),
        (((1,), (1,)), ((), ())),
        preferred_element_type=F32,
    )
    ids = meta[:TOPK]
    weights = (meta[TOPK : 2 * TOPK] + meta[2 * TOPK : 3 * TOPK]) + meta[3 * TOPK : 4 * TOPK]
    early = lax.broadcasted_iota(jnp.int32, (lanes, lanes), 0)
    late = lax.broadcasted_iota(jnp.int32, (lanes, lanes), 1)
    before = ((early // tokens == late // tokens) & (early < late)).astype(F32).astype(BF16)

    row = lax.broadcasted_iota(jnp.int32, (count, lanes), 0)
    block = lax.broadcasted_iota(jnp.int32, (count, lanes), 1) // tokens
    copy = (row % 2).astype(F32)

    def choose(table, entry, seat, senses):
        base = jnp.zeros((count, lanes), jnp.int32)
        wanted = jnp.zeros((count, lanes), jnp.int32)
        for i, (step, source) in enumerate(table):
            goals = [lax.rem(plane + sense * step + PLANES, PLANES) * SEATS for sense in senses]
            goal = goals[0] if len(goals) == 1 else jnp.where(seat % 2 == 0, goals[0], goals[1])
            base = jnp.where(entry == i, goal, base)
            wanted = jnp.where(entry == i, source, wanted)
        expert = (base + seat).astype(F32)
        hit = jnp.zeros((count, lanes), F32)
        scale = jnp.zeros((count, lanes), F32)
        for k in range(TOPK):
            found = ids[k : k + 1, :] == expert
            hit = jnp.where(found, 1.0, hit)
            scale = jnp.where(found, weights[k : k + 1, :], scale)
        rank = jnp.dot(hit.astype(BF16), before, preferred_element_type=F32)
        chosen = (hit > 0.5) & (jnp.abs(rank - copy) < 0.5) & (block == wanted)
        chosen = jnp.where(chosen, 1.0, 0.0)
        return chosen.astype(BF16), jnp.sum(chosen * scale, axis=1, keepdims=True)

    near, near_weight = choose(NEAR, (row // 2) % 8, row // GROUP, (1, -1))
    far, far_weight = choose(FAR, row // GROUP, (row // 2) % SEATS, (sign,))
    for part in range(parts):
        cut = pl.ds(part * part_width, part_width)
        tile = jnp.concatenate([ref[:, cut] for ref in refs], axis=0)
        rows = jnp.dot(far, tile, preferred_element_type=F32)
        rows = (far_weight * rows).astype(BF16)
        at = 0
        for ref, size in zip(far_refs, CUTS, strict=True):
            ref[:, cut] = rows[at : at + size]
            at += size
        rows = jnp.dot(near, tile, preferred_element_type=F32)
        near_ref[part] = (near_weight * rows).astype(BF16)


def picked(plane, sign, own, behind, ahead, parts):
    width = own.shape[1] - META
    shapes = [(parts, SEATS * GROUP, width // parts)] + [(size, width) for size in CUTS]
    return pl.pallas_call(
        pick_kernel,
        in_specs=[pl.BlockSpec(memory_space=pltpu.SMEM)] + [pl.BlockSpec(memory_space=pltpu.VMEM)] * 3,
        out_shape=[jax.ShapeDtypeStruct(shape, BF16) for shape in shapes],
        compiler_params=SMALL,
    )(jnp.stack([plane, sign]).astype(jnp.int32), own, behind, ahead)


def join_kernel(*refs):
    *in_refs, out_ref = refs
    parts, count, width = out_ref.shape
    to = lax.broadcasted_iota(jnp.int32, (count, count), 0)
    at = lax.broadcasted_iota(jnp.int32, (count, count), 1)
    seat, entry, copy = to // GROUP, (to // 2) % 8, to % 2
    move = (at == entry * GROUP + seat * 2 + copy).astype(F32).astype(BF16)
    for part in range(parts):
        cut = pl.ds(part * width, width)
        rows = jnp.concatenate([ref[:, cut] for ref in in_refs], axis=0)
        out_ref[part] = jnp.dot(move, rows, preferred_element_type=F32).astype(BF16)


def join(pieces, parts):
    rows = sum(piece.shape[0] for piece in pieces)
    return pl.pallas_call(
        join_kernel,
        out_shape=jax.ShapeDtypeStruct((parts, rows, pieces[0].shape[1] // parts), BF16),
        compiler_params=SMALL,
    )(*pieces)


def shift(array, step):
    pairs = []
    for z in range(PLANES):
        for core in range(2):
            goal = (z + (step if core == 0 else -step)) % PLANES
            pairs.append((z * 2 + core, goal * 2 + core))
    return lax.ppermute(array, ("z", "core"), pairs)


def gathered(array, axis):
    count = lax.axis_size(axis)
    copies = jnp.broadcast_to(array[None], (count, *array.shape))
    return lax.all_to_all(copies, axis, split_axis=0, concat_axis=0, tiled=True)


def exchanged(array):
    array = array.reshape(-1, GROUP, array.shape[2])
    return lax.all_to_all(array, ("dp", "x", "core"), split_axis=0, concat_axis=0, tiled=True)


def factor_moves(plane, sign, slots):
    moves = []
    for low, high in ((0, 8), (8, 12), (12, 16), (16, 24)):
        span = SLOTS[low:high]
        size = len(span)
        to = np.arange(SEATS * size * 2)
        seat, entry, copy = to // (size * 2), (to // 2) % size, to % 2
        ahead = np.array([0 if s is None else s[0] for s in span])[entry] * (1 - 2 * (seat % 2))
        behind = np.array([0 if s is None else s[1] for s in span])[entry]
        real = np.array([s is not None for s in span])[entry]
        moves.append(np.stack([ahead, behind, seat * 2 + copy, real]))
    ahead, behind, within, real = np.concatenate(moves, axis=1).astype(np.int32)
    slot = (plane + ahead - sign * behind + 2 * PLANES) % PLANES * GROUP + within
    same = slot[:, None] == jnp.arange(slots, dtype=jnp.int32)[None, :]
    return (same & (real[:, None] > 0)).astype(BF16)


def cut_kernel(in_ref, up_ref, down_ref):
    half = up_ref.shape[1]
    up_ref[...] = in_ref[:, :half]
    down_ref[...] = in_ref[:, half:]


def halves(array):
    count, rows, width = array.shape
    steps = 4

    def spec(size):
        return pl.BlockSpec((count // steps, size, width), lambda i: (i, 0, 0))

    shape = jax.ShapeDtypeStruct((count, rows // 2, width), array.dtype)
    return pl.pallas_call(
        cut_kernel,
        grid=(steps,),
        in_specs=[spec(rows)],
        out_specs=[spec(rows // 2)] * 2,
        out_shape=[shape] * 2,
        compiler_params=SMALL,
    )(array)


def order_kernel(move_ref, reduced_ref, *out_refs):
    for replica in range(reduced_ref.shape[0]):
        rows = jnp.dot(move_ref[...], reduced_ref[replica], preferred_element_type=F32)
        at = 0
        for ref in out_refs:
            ref[replica] = rows[at : at + ref.shape[1]].astype(BF16)
            at += ref.shape[1]


def ordered(moves, reduced):
    replicas, _, rank = reduced.shape
    sizes = [2 * SEATS * count for count in (8, 4, 4, 8)]
    return pl.pallas_call(
        order_kernel,
        out_shape=[jax.ShapeDtypeStruct((replicas, size, rank), BF16) for size in sizes],
        compiler_params=SMALL,
    )(moves, reduced)


def layer(grad_out, expert_ids, route_weights, hidden_act, projection):
    parts = lax.axis_size("dp")
    tokens, width = grad_out.shape
    rank = projection.shape[2]
    plane, core = lax.axis_index("z"), lax.axis_index("core")
    sign = 1 - 2 * core
    own = pl.pallas_call(
        pack_kernel,
        out_shape=jax.ShapeDtypeStruct((tokens, width + META), BF16),
    )(grad_out, expert_ids.T, route_weights.T)
    behind, ahead = shift(own, LEAP), shift(own, -LEAP)

    basis = gathered(projection[0], "dp").reshape(-1, rank)
    moves = factor_moves(plane, sign, hidden_act.shape[2])
    basis, moves = lax.optimization_barrier((basis, moves))
    reduced = jnp.dot(hidden_act[0, 0], basis, preferred_element_type=F32).astype(BF16)
    reduced = gathered(reduced, "dp")

    near, stay, up2, down2, up3 = picked(plane, sign, own, behind, ahead, parts)
    up2, down2, up3 = shift(up2, 2), shift(down2, -2), shift(up3, 3)
    near, reduced = lax.optimization_barrier((near, reduced))
    near = exchanged(near)
    factors = ordered(moves, reduced)
    far = join([stay, up2, down2, up3], parts)
    up1, down1 = halves(near)
    far, up1 = lax.optimization_barrier((far, up1))
    far = exchanged(far)
    up1, down1 = shift(up1, 1), shift(down1, -1)
    total = None
    for piece, factor in zip((near, up1, down1, far), factors, strict=True):
        share = lax.dot_general(
            piece.reshape(-1, piece.shape[2]),
            factor.reshape(-1, rank),
            (((0,), (0,)), ((), ())),
            preferred_element_type=F32,
        )
        total = share if total is None else total + share
    return total.astype(BF16)[None]


def solution(mesh):
    names = ("dp", "z", "x", "core")
    fine = Mesh(mesh.devices.reshape(mesh.shape["dp"], PLANES, -1, 2), names)
    devices = ("z", "x", "core")
    in_specs = (
        P(names, None),
        P(names, None),
        P(names, None),
        P("dp", devices, None, None),
        P(devices, "dp", None),
    )
    out_specs = P(devices, "dp", None)
    return jax.shard_map(layer, mesh=fine, in_specs=in_specs, out_specs=out_specs, check_vma=False)
```

```python
import numpy as np

import jax
import jax.numpy as jnp
from jax import lax
from jax.experimental import pallas as pl
from jax.experimental.pallas import tpu as pltpu
from jax.sharding import Mesh, PartitionSpec as P


PLANES = 16
SEATS = 8
LEAP = 4
META = 128
TOPK = 8
GROUP = 2 * SEATS
F32, BF16 = jnp.float32, jnp.bfloat16
SMALL = pltpu.CompilerParams(vmem_limit_bytes=12 * 1024 * 1024)

START = (0, -LEAP, LEAP)
NEAR = ((1, 0), (1, 1), (1, 2), (0, 0), (-1, 0), (-1, 1), (-1, 2), (0, 1))
FAR = ((0, 2), (2, 0), (2, 1), (-2, 0), (-2, 2), (3, 1), (-3, 2), (4, 1))
CUTS = (GROUP, 2 * GROUP, 2 * GROUP, GROUP, GROUP, GROUP)


def origins(table, moved):
    return [(START[block], step) if step == moved else None for step, block in table]


SLOTS = (
    origins(NEAR, 0)
    + origins(NEAR[:4], 1)
    + origins(NEAR[4:], -1)
    + [(START[block] - step, 0) for step, block in FAR]
)


def pack_kernel(grad_ref, ids_ref, weight_ref, out_ref):
    tokens, width = grad_ref.shape
    high = weight_ref[...].astype(BF16).astype(F32)
    rest = weight_ref[...] - high
    middle = rest.astype(BF16).astype(F32)
    low = rest - middle
    parts = [ids_ref[...].astype(F32), high, middle, low]
    used = sum(part.shape[0] for part in parts)
    meta = jnp.concatenate(parts + [jnp.zeros((META - used, tokens), F32)], axis=0)
    same = lax.broadcasted_iota(jnp.int32, (tokens, tokens), 0) == lax.broadcasted_iota(
        jnp.int32, (tokens, tokens), 1
    )
    turned = lax.dot_general(
        same.astype(F32).astype(BF16),
        meta.astype(BF16),
        (((1,), (1,)), ((), ())),
        preferred_element_type=F32,
    )
    out_ref[:, :width] = grad_ref[...]
    out_ref[:, width:] = turned.astype(BF16)


def pick_kernel(place_ref, own_ref, behind_ref, ahead_ref, near_out, *rest):
    far_outs, (near_ref, far_ref, sems) = rest[: len(CUTS)], rest[len(CUTS) :]
    refs = (own_ref, behind_ref, ahead_ref)
    tokens = own_ref.shape[0]
    width = own_ref.shape[1] - META
    lanes = tokens * len(refs)
    parts, count, part_width = near_ref.shape
    plane, sign = place_ref[0], place_ref[1]

    same = lax.broadcasted_iota(jnp.int32, (META, META), 0) == lax.broadcasted_iota(
        jnp.int32, (META, META), 1
    )
    meta = lax.dot_general(
        same.astype(F32).astype(BF16),
        jnp.concatenate([ref[:, width:] for ref in refs], axis=0),
        (((1,), (1,)), ((), ())),
        preferred_element_type=F32,
    )
    ids = meta[:TOPK]
    weights = (meta[TOPK : 2 * TOPK] + meta[2 * TOPK : 3 * TOPK]) + meta[3 * TOPK : 4 * TOPK]
    early = lax.broadcasted_iota(jnp.int32, (lanes, lanes), 0)
    late = lax.broadcasted_iota(jnp.int32, (lanes, lanes), 1)
    before = ((early // tokens == late // tokens) & (early < late)).astype(F32).astype(BF16)

    row = lax.broadcasted_iota(jnp.int32, (count, lanes), 0)
    block = lax.broadcasted_iota(jnp.int32, (count, lanes), 1) // tokens
    copy = (row % 2).astype(F32)

    def choose(table, entry, seat, senses):
        base = jnp.zeros((count, lanes), jnp.int32)
        wanted = jnp.zeros((count, lanes), jnp.int32)
        for i, (step, source) in enumerate(table):
            goals = [lax.rem(plane + sense * step + PLANES, PLANES) * SEATS for sense in senses]
            goal = goals[0] if len(goals) == 1 else jnp.where(seat % 2 == 0, goals[0], goals[1])
            base = jnp.where(entry == i, goal, base)
            wanted = jnp.where(entry == i, source, wanted)
        expert = (base + seat).astype(F32)
        hit = jnp.zeros((count, lanes), F32)
        scale = jnp.zeros((count, lanes), F32)
        for k in range(TOPK):
            found = ids[k : k + 1, :] == expert
            hit = jnp.where(found, 1.0, hit)
            scale = jnp.where(found, weights[k : k + 1, :], scale)
        rank = jnp.dot(hit.astype(BF16), before, preferred_element_type=F32)
        chosen = (hit > 0.5) & (jnp.abs(rank - copy) < 0.5) & (block == wanted)
        chosen = jnp.where(chosen, 1.0, 0.0)
        return chosen.astype(BF16), jnp.sum(chosen * scale, axis=1, keepdims=True)

    near, near_weight = choose(NEAR, (row // 2) % 8, row // GROUP, (1, -1))
    far, far_weight = choose(FAR, row // GROUP, (row // 2) % SEATS, (sign,))
    copies = []

    def send(source, goal):
        copies.append(pltpu.make_async_copy(source, goal, sems.at[len(copies)]))
        copies[-1].start()

    for part in range(parts):
        cut = pl.ds(part * part_width, part_width)
        tile = jnp.concatenate([ref[:, cut] for ref in refs], axis=0)
        rows = jnp.dot(far, tile, preferred_element_type=F32)
        far_ref[:, cut] = (far_weight * rows).astype(BF16)
        at = 0
        for out, size in zip(far_outs, CUTS, strict=True):
            send(far_ref.at[pl.ds(at, size), cut], out.at[:, cut])
            at += size
        rows = jnp.dot(near, tile, preferred_element_type=F32)
        near_ref[part] = (near_weight * rows).astype(BF16)
        send(near_ref.at[part], near_out.at[part])
    for copy_out in copies:
        copy_out.wait()


def picked(plane, sign, own, behind, ahead, parts):
    width = own.shape[1] - META
    shapes = [(parts, SEATS * GROUP, width // parts)] + [(size, width) for size in CUTS]
    return pl.pallas_call(
        pick_kernel,
        in_specs=[pl.BlockSpec(memory_space=pltpu.SMEM)] + [pl.BlockSpec(memory_space=pltpu.VMEM)] * 3,
        out_specs=[pl.BlockSpec(memory_space=pltpu.HBM)] * len(shapes),
        out_shape=[jax.ShapeDtypeStruct(shape, BF16) for shape in shapes],
        scratch_shapes=[
            pltpu.VMEM(shapes[0], BF16),
            pltpu.VMEM((sum(CUTS), width), BF16),
            pltpu.SemaphoreType.DMA((parts * len(shapes),)),
        ],
        compiler_params=SMALL,
    )(jnp.stack([plane, sign]).astype(jnp.int32), own, behind, ahead)


def join_kernel(*refs):
    *in_refs, out_ref = refs
    parts, count, width = out_ref.shape
    to = lax.broadcasted_iota(jnp.int32, (count, count), 0)
    at = lax.broadcasted_iota(jnp.int32, (count, count), 1)
    seat, entry, copy = to // GROUP, (to // 2) % 8, to % 2
    move = (at == entry * GROUP + seat * 2 + copy).astype(F32).astype(BF16)
    for part in range(parts):
        cut = pl.ds(part * width, width)
        rows = jnp.concatenate([ref[:, cut] for ref in in_refs], axis=0)
        out_ref[part] = jnp.dot(move, rows, preferred_element_type=F32).astype(BF16)


def join(pieces, parts):
    rows = sum(piece.shape[0] for piece in pieces)
    return pl.pallas_call(
        join_kernel,
        out_shape=jax.ShapeDtypeStruct((parts, rows, pieces[0].shape[1] // parts), BF16),
        compiler_params=SMALL,
    )(*pieces)


def shift(array, step):
    pairs = []
    for z in range(PLANES):
        for core in range(2):
            goal = (z + (step if core == 0 else -step)) % PLANES
            pairs.append((z * 2 + core, goal * 2 + core))
    return lax.ppermute(array, ("z", "core"), pairs)


def gathered(array, axis):
    count = lax.axis_size(axis)
    copies = jnp.broadcast_to(array[None], (count, *array.shape))
    return lax.all_to_all(copies, axis, split_axis=0, concat_axis=0, tiled=True)


def exchanged(array):
    array = array.reshape(-1, GROUP, array.shape[2])
    return lax.all_to_all(array, ("dp", "x", "core"), split_axis=0, concat_axis=0, tiled=True)


def factor_moves(plane, sign, slots):
    moves = []
    for low, high in ((0, 8), (8, 12), (12, 16), (16, 24)):
        span = SLOTS[low:high]
        size = len(span)
        to = np.arange(SEATS * size * 2)
        seat, entry, copy = to // (size * 2), (to // 2) % size, to % 2
        ahead = np.array([0 if s is None else s[0] for s in span])[entry] * (1 - 2 * (seat % 2))
        behind = np.array([0 if s is None else s[1] for s in span])[entry]
        real = np.array([s is not None for s in span])[entry]
        moves.append(np.stack([ahead, behind, seat * 2 + copy, real]))
    ahead, behind, within, real = np.concatenate(moves, axis=1).astype(np.int32)
    slot = (plane + ahead - sign * behind + 2 * PLANES) % PLANES * GROUP + within
    same = slot[:, None] == jnp.arange(slots, dtype=jnp.int32)[None, :]
    return (same & (real[:, None] > 0)).astype(BF16)


def cut_kernel(in_ref, up_ref, down_ref, sems):
    half = up_ref.shape[1]
    up = pltpu.make_async_copy(in_ref.at[:, pl.ds(0, half)], up_ref, sems.at[0])
    down = pltpu.make_async_copy(in_ref.at[:, pl.ds(half, half)], down_ref, sems.at[1])
    up.start()
    down.start()
    up.wait()
    down.wait()


def halves(array):
    count, rows, width = array.shape
    shape = jax.ShapeDtypeStruct((count, rows // 2, width), array.dtype)
    return pl.pallas_call(
        cut_kernel,
        in_specs=[pl.BlockSpec(memory_space=pltpu.VMEM)],
        out_specs=[pl.BlockSpec(memory_space=pltpu.HBM)] * 2,
        out_shape=[shape] * 2,
        scratch_shapes=[pltpu.SemaphoreType.DMA((2,))],
        compiler_params=SMALL,
    )(array)


def order_kernel(move_ref, reduced_ref, *out_refs):
    for replica in range(reduced_ref.shape[0]):
        rows = jnp.dot(move_ref[...], reduced_ref[replica], preferred_element_type=F32)
        at = 0
        for ref in out_refs:
            ref[replica] = rows[at : at + ref.shape[1]].astype(BF16)
            at += ref.shape[1]


def ordered(moves, reduced):
    replicas, _, rank = reduced.shape
    sizes = [2 * SEATS * count for count in (8, 4, 4, 8)]
    return pl.pallas_call(
        order_kernel,
        out_shape=[jax.ShapeDtypeStruct((replicas, size, rank), BF16) for size in sizes],
        compiler_params=SMALL,
    )(moves, reduced)


def layer(grad_out, expert_ids, route_weights, hidden_act, projection):
    parts = lax.axis_size("dp")
    tokens, width = grad_out.shape
    rank = projection.shape[2]
    plane, core = lax.axis_index("z"), lax.axis_index("core")
    sign = 1 - 2 * core
    own = pl.pallas_call(
        pack_kernel,
        out_shape=jax.ShapeDtypeStruct((tokens, width + META), BF16),
    )(grad_out, expert_ids.T, route_weights.T)
    behind, ahead = shift(own, LEAP), shift(own, -LEAP)

    basis = gathered(projection[0], "dp").reshape(-1, rank)
    moves = factor_moves(plane, sign, hidden_act.shape[2])
    basis, moves = lax.optimization_barrier((basis, moves))
    reduced = jnp.dot(hidden_act[0, 0], basis, preferred_element_type=F32).astype(BF16)
    reduced = gathered(reduced, "dp")

    near, stay, up2, down2, up3, down3, up4 = picked(plane, sign, own, behind, ahead, parts)
    up2, down2 = shift(up2, 2), shift(down2, -2)
    up3, down3, up4 = shift(up3, 3), shift(down3, -3), shift(up4, 4)
    near, reduced = lax.optimization_barrier((near, reduced))
    near = exchanged(near)
    factors = ordered(moves, reduced)
    far = join([stay, up2, down2, up3, down3, up4], parts)
    up1, down1 = halves(near)
    far, up1 = lax.optimization_barrier((far, up1))
    far = exchanged(far)
    up1, down1 = shift(up1, 1), shift(down1, -1)
    total = None
    for piece, factor in zip((near, up1, down1, far), factors, strict=True):
        share = lax.dot_general(
            piece.reshape(-1, piece.shape[2]),
            factor.reshape(-1, rank),
            (((0,), (0,)), ((), ())),
            preferred_element_type=F32,
        )
        total = share if total is None else total + share
    return total.astype(BF16)[None]


def solution(mesh):
    names = ("dp", "z", "x", "core")
    fine = Mesh(mesh.devices.reshape(mesh.shape["dp"], PLANES, -1, 2), names)
    devices = ("z", "x", "core")
    in_specs = (
        P(names, None),
        P(names, None),
        P(names, None),
        P("dp", devices, None, None),
        P(devices, "dp", None),
    )
    out_specs = P(devices, "dp", None)
    return jax.shard_map(layer, mesh=fine, in_specs=in_specs, out_specs=out_specs, check_vma=False)
```

```python
import numpy as np

import jax
import jax.numpy as jnp
from jax import lax
from jax.experimental import pallas as pl
from jax.experimental.pallas import tpu as pltpu
from jax.sharding import Mesh, PartitionSpec as P


PLANES = 16
SEATS = 8
LEAP = 5
META = 128
TOPK = 8
GROUP = 2 * SEATS
F32, BF16 = jnp.float32, jnp.bfloat16
SMALL = pltpu.CompilerParams(vmem_limit_bytes=12 * 1024 * 1024)

START = (0, -LEAP, LEAP)
NEAR = ((2, 0), (2, 1), (2, 2), (0, 0), (-2, 0), (-2, 1), (-2, 2), (0, 1))
FAR = ((0, 2), (1, 0), (1, 1), (1, 2), (-1, 0), (-1, 1), (-1, 2), (3, 1))
CUTS = (GROUP, 3 * GROUP, 3 * GROUP, GROUP)
HALVES = ((0, 3), (4, 7))


def origins(table, moved):
    return [(START[block], step) if step == moved else None for step, block in table]


SLOTS = (
    origins(NEAR, 0)
    + origins(NEAR[slice(*HALVES[0])], 2)
    + origins(NEAR[slice(*HALVES[1])], -2)
    + [(START[block] - step, 0) for step, block in FAR]
)


def pack_kernel(grad_ref, ids_ref, weight_ref, out_ref):
    tokens, width = grad_ref.shape
    high = weight_ref[...].astype(BF16).astype(F32)
    rest = weight_ref[...] - high
    middle = rest.astype(BF16).astype(F32)
    low = rest - middle
    parts = [ids_ref[...].astype(F32), high, middle, low]
    used = sum(part.shape[0] for part in parts)
    meta = jnp.concatenate(parts + [jnp.zeros((META - used, tokens), F32)], axis=0)
    same = lax.broadcasted_iota(jnp.int32, (tokens, tokens), 0) == lax.broadcasted_iota(
        jnp.int32, (tokens, tokens), 1
    )
    turned = lax.dot_general(
        same.astype(F32).astype(BF16),
        meta.astype(BF16),
        (((1,), (1,)), ((), ())),
        preferred_element_type=F32,
    )
    out_ref[:, :width] = grad_ref[...]
    out_ref[:, width:] = turned.astype(BF16)


def pick_kernel(place_ref, own_ref, behind_ref, ahead_ref, near_ref, *far_refs):
    refs = (own_ref, behind_ref, ahead_ref)
    tokens = own_ref.shape[0]
    width = own_ref.shape[1] - META
    lanes = tokens * len(refs)
    parts, count, part_width = near_ref.shape
    plane, sign = place_ref[0], place_ref[1]

    same = lax.broadcasted_iota(jnp.int32, (META, META), 0) == lax.broadcasted_iota(
        jnp.int32, (META, META), 1
    )
    meta = lax.dot_general(
        same.astype(F32).astype(BF16),
        jnp.concatenate([ref[:, width:] for ref in refs], axis=0),
        (((1,), (1,)), ((), ())),
        preferred_element_type=F32,
    )
    ids = meta[:TOPK]
    weights = (meta[TOPK : 2 * TOPK] + meta[2 * TOPK : 3 * TOPK]) + meta[3 * TOPK : 4 * TOPK]
    early = lax.broadcasted_iota(jnp.int32, (lanes, lanes), 0)
    late = lax.broadcasted_iota(jnp.int32, (lanes, lanes), 1)
    before = ((early // tokens == late // tokens) & (early < late)).astype(F32).astype(BF16)

    row = lax.broadcasted_iota(jnp.int32, (count, lanes), 0)
    block = lax.broadcasted_iota(jnp.int32, (count, lanes), 1) // tokens
    copy = (row % 2).astype(F32)

    def choose(table, entry, seat, senses):
        base = jnp.zeros((count, lanes), jnp.int32)
        wanted = jnp.zeros((count, lanes), jnp.int32)
        for i, (step, source) in enumerate(table):
            goals = [lax.rem(plane + sense * step + PLANES, PLANES) * SEATS for sense in senses]
            goal = goals[0] if len(goals) == 1 else jnp.where(seat % 2 == 0, goals[0], goals[1])
            base = jnp.where(entry == i, goal, base)
            wanted = jnp.where(entry == i, source, wanted)
        expert = (base + seat).astype(F32)
        hit = jnp.zeros((count, lanes), F32)
        scale = jnp.zeros((count, lanes), F32)
        for k in range(TOPK):
            found = ids[k : k + 1, :] == expert
            hit = jnp.where(found, 1.0, hit)
            scale = jnp.where(found, weights[k : k + 1, :], scale)
        rank = jnp.dot(hit.astype(BF16), before, preferred_element_type=F32)
        chosen = (hit > 0.5) & (jnp.abs(rank - copy) < 0.5) & (block == wanted)
        chosen = jnp.where(chosen, 1.0, 0.0)
        return chosen.astype(BF16), jnp.sum(chosen * scale, axis=1, keepdims=True)

    near, near_weight = choose(NEAR, (row // 2) % 8, row // GROUP, (1, -1))
    far, far_weight = choose(FAR, row // GROUP, (row // 2) % SEATS, (sign,))
    for part in range(parts):
        cut = pl.ds(part * part_width, part_width)
        tile = jnp.concatenate([ref[:, cut] for ref in refs], axis=0)
        rows = jnp.dot(far, tile, preferred_element_type=F32)
        rows = (far_weight * rows).astype(BF16)
        at = 0
        for ref, size in zip(far_refs, CUTS, strict=True):
            ref[:, cut] = rows[at : at + size]
            at += size
        rows = jnp.dot(near, tile, preferred_element_type=F32)
        near_ref[part] = (near_weight * rows).astype(BF16)


def picked(plane, sign, own, behind, ahead, parts):
    width = own.shape[1] - META
    shapes = [(parts, SEATS * GROUP, width // parts)] + [(size, width) for size in CUTS]
    return pl.pallas_call(
        pick_kernel,
        in_specs=[pl.BlockSpec(memory_space=pltpu.SMEM)] + [pl.BlockSpec(memory_space=pltpu.VMEM)] * 3,
        out_shape=[jax.ShapeDtypeStruct(shape, BF16) for shape in shapes],
        compiler_params=SMALL,
    )(jnp.stack([plane, sign]).astype(jnp.int32), own, behind, ahead)


def join_kernel(*refs):
    *in_refs, out_ref = refs
    parts, count, width = out_ref.shape
    to = lax.broadcasted_iota(jnp.int32, (count, count), 0)
    at = lax.broadcasted_iota(jnp.int32, (count, count), 1)
    seat, entry, copy = to // GROUP, (to // 2) % 8, to % 2
    move = (at == entry * GROUP + seat * 2 + copy).astype(F32).astype(BF16)
    for part in range(parts):
        cut = pl.ds(part * width, width)
        rows = jnp.concatenate([ref[:, cut] for ref in in_refs], axis=0)
        out_ref[part] = jnp.dot(move, rows, preferred_element_type=F32).astype(BF16)


def join(pieces, parts):
    rows = sum(piece.shape[0] for piece in pieces)
    return pl.pallas_call(
        join_kernel,
        out_shape=jax.ShapeDtypeStruct((parts, rows, pieces[0].shape[1] // parts), BF16),
        compiler_params=SMALL,
    )(*pieces)


def shift(array, step):
    pairs = []
    for z in range(PLANES):
        for core in range(2):
            goal = (z + (step if core == 0 else -step)) % PLANES
            pairs.append((z * 2 + core, goal * 2 + core))
    return lax.ppermute(array, ("z", "core"), pairs)


def gathered(array, axis):
    count = lax.axis_size(axis)
    copies = jnp.broadcast_to(array[None], (count, *array.shape))
    return lax.all_to_all(copies, axis, split_axis=0, concat_axis=0, tiled=True)


def exchanged(array):
    array = array.reshape(-1, GROUP, array.shape[2])
    return lax.all_to_all(array, ("dp", "x", "core"), split_axis=0, concat_axis=0, tiled=True)


def factor_moves(plane, sign, slots):
    moves = []
    for low, high in ((0, 8), (8, 11), (11, 14), (14, 22)):
        span = SLOTS[low:high]
        size = len(span)
        to = np.arange(SEATS * size * 2)
        seat, entry, copy = to // (size * 2), (to // 2) % size, to % 2
        ahead = np.array([0 if s is None else s[0] for s in span])[entry] * (1 - 2 * (seat % 2))
        behind = np.array([0 if s is None else s[1] for s in span])[entry]
        real = np.array([s is not None for s in span])[entry]
        moves.append(np.stack([ahead, behind, seat * 2 + copy, real]))
    ahead, behind, within, real = np.concatenate(moves, axis=1).astype(np.int32)
    slot = (plane + ahead - sign * behind + 2 * PLANES) % PLANES * GROUP + within
    same = slot[:, None] == jnp.arange(slots, dtype=jnp.int32)[None, :]
    return (same & (real[:, None] > 0)).astype(BF16)


def cut_kernel(in_ref, up_ref, down_ref):
    steps = 2
    chunk = in_ref.shape[0] // steps
    for ref, (low, high) in zip((up_ref, down_ref), HALVES, strict=True):
        size = 2 * (high - low)
        count = chunk // GROUP * size
        row = lax.broadcasted_iota(jnp.int32, (count, chunk), 0)
        goal = lax.broadcasted_iota(jnp.int32, (count, chunk), 1)
        source = (row * (65536 // size + 1)) >> 16
        move = (goal == source * GROUP + 2 * low + row - source * size).astype(F32).astype(BF16)
        for step in range(steps):
            rows = jnp.dot(
                move, in_ref[step * chunk : (step + 1) * chunk], preferred_element_type=F32
            )
            ref[step * count : (step + 1) * count] = rows.astype(BF16)


def halves(array):
    count, rows, width = array.shape
    shapes = [
        jax.ShapeDtypeStruct((count * 2 * (high - low), width), array.dtype) for low, high in HALVES
    ]
    return pl.pallas_call(cut_kernel, out_shape=shapes, compiler_params=SMALL)(
        array.reshape(count * rows, width)
    )


def order_kernel(move_ref, reduced_ref, *out_refs):
    for replica in range(reduced_ref.shape[0]):
        rows = jnp.dot(move_ref[...], reduced_ref[replica], preferred_element_type=F32)
        at = 0
        for ref in out_refs:
            ref[replica] = rows[at : at + ref.shape[1]].astype(BF16)
            at += ref.shape[1]


def ordered(moves, reduced):
    replicas, _, rank = reduced.shape
    sizes = [2 * SEATS * count for count in (8, 3, 3, 8)]
    return pl.pallas_call(
        order_kernel,
        out_shape=[jax.ShapeDtypeStruct((replicas, size, rank), BF16) for size in sizes],
        compiler_params=SMALL,
    )(moves, reduced)


def layer(grad_out, expert_ids, route_weights, hidden_act, projection):
    parts = lax.axis_size("dp")
    tokens, width = grad_out.shape
    rank = projection.shape[2]
    plane, core = lax.axis_index("z"), lax.axis_index("core")
    sign = 1 - 2 * core
    own = pl.pallas_call(
        pack_kernel,
        out_shape=jax.ShapeDtypeStruct((tokens, width + META), BF16),
    )(grad_out, expert_ids.T, route_weights.T)
    behind, ahead = shift(own, LEAP), shift(own, -LEAP)

    basis = gathered(projection[0], "dp").reshape(-1, rank)
    moves = factor_moves(plane, sign, hidden_act.shape[2])
    basis, moves = lax.optimization_barrier((basis, moves))
    reduced = jnp.dot(hidden_act[0, 0], basis, preferred_element_type=F32).astype(BF16)
    reduced = gathered(reduced, "dp")

    near, stay, up1, down1, up3 = picked(plane, sign, own, behind, ahead, parts)
    up1, down1, up3 = shift(up1, 1), shift(down1, -1), shift(up3, 3)
    near, reduced = lax.optimization_barrier((near, reduced))
    near = exchanged(near)
    factors = ordered(moves, reduced)
    far = join([stay, up1, down1, up3], parts)
    far = exchanged(far)
    up2, down2 = halves(near)
    up2, down2 = shift(up2, 2), shift(down2, -2)
    total = None
    for piece, factor in zip((near, up2, down2, far), factors, strict=True):
        share = lax.dot_general(
            piece.reshape(-1, piece.shape[-1]),
            factor.reshape(-1, rank),
            (((0,), (0,)), ((), ())),
            preferred_element_type=F32,
        )
        total = share if total is None else total + share
    return total.astype(BF16)[None]


def solution(mesh):
    names = ("dp", "z", "x", "core")
    fine = Mesh(mesh.devices.reshape(mesh.shape["dp"], PLANES, -1, 2), names)
    devices = ("z", "x", "core")
    in_specs = (
        P(names, None),
        P(names, None),
        P(names, None),
        P("dp", devices, None, None),
        P(devices, "dp", None),
    )
    out_specs = P(devices, "dp", None)
    return jax.shard_map(layer, mesh=fine, in_specs=in_specs, out_specs=out_specs, check_vma=False)
```

```python
import numpy as np

import jax
import jax.numpy as jnp
from jax import lax
from jax.experimental import pallas as pl
from jax.experimental.pallas import tpu as pltpu
from jax.sharding import Mesh, PartitionSpec as P


PLANES = 16
SEATS = 8
LEAP = 5
META = 128
TOPK = 8
GROUP = 2 * SEATS
F32, BF16 = jnp.float32, jnp.bfloat16
SMALL = pltpu.CompilerParams(vmem_limit_bytes=12 * 1024 * 1024)

START = (0, -LEAP, LEAP)
NEAR = ((1, 0), (1, 1), (1, 2), (0, 0), (-1, 0), (-1, 1), (-1, 2), (0, 1))
FAR = ((0, 2), (2, 0), (2, 1), (2, 2), (-2, 0), (-2, 1), (-2, 2), (3, 1))
CUTS = (GROUP, 3 * GROUP, 3 * GROUP, GROUP)
HALVES = ((0, 3), (4, 7))


def origins(table, moved):
    return [(START[block], step) if step == moved else None for step, block in table]


SLOTS = (
    origins(NEAR, 0)
    + origins(NEAR[slice(*HALVES[0])], 1)
    + origins(NEAR[slice(*HALVES[1])], -1)
    + [(START[block] - step, 0) for step, block in FAR]
)


def pack_kernel(grad_ref, ids_ref, weight_ref, out_ref):
    tokens, width = grad_ref.shape
    high = weight_ref[...].astype(BF16).astype(F32)
    rest = weight_ref[...] - high
    middle = rest.astype(BF16).astype(F32)
    low = rest - middle
    parts = [ids_ref[...].astype(F32), high, middle, low]
    used = sum(part.shape[0] for part in parts)
    meta = jnp.concatenate(parts + [jnp.zeros((META - used, tokens), F32)], axis=0)
    same = lax.broadcasted_iota(jnp.int32, (tokens, tokens), 0) == lax.broadcasted_iota(
        jnp.int32, (tokens, tokens), 1
    )
    turned = lax.dot_general(
        same.astype(F32).astype(BF16),
        meta.astype(BF16),
        (((1,), (1,)), ((), ())),
        preferred_element_type=F32,
    )
    out_ref[:, :width] = grad_ref[...]
    out_ref[:, width:] = turned.astype(BF16)


def pick_kernel(place_ref, own_ref, behind_ref, ahead_ref, near_ref, *far_refs):
    refs = (own_ref, behind_ref, ahead_ref)
    tokens = own_ref.shape[0]
    width = own_ref.shape[1] - META
    lanes = tokens * len(refs)
    parts, count, part_width = near_ref.shape
    plane, sign = place_ref[0], place_ref[1]

    same = lax.broadcasted_iota(jnp.int32, (META, META), 0) == lax.broadcasted_iota(
        jnp.int32, (META, META), 1
    )
    meta = lax.dot_general(
        same.astype(F32).astype(BF16),
        jnp.concatenate([ref[:, width:] for ref in refs], axis=0),
        (((1,), (1,)), ((), ())),
        preferred_element_type=F32,
    )
    ids = meta[:TOPK]
    weights = (meta[TOPK : 2 * TOPK] + meta[2 * TOPK : 3 * TOPK]) + meta[3 * TOPK : 4 * TOPK]
    early = lax.broadcasted_iota(jnp.int32, (lanes, lanes), 0)
    late = lax.broadcasted_iota(jnp.int32, (lanes, lanes), 1)
    before = ((early // tokens == late // tokens) & (early < late)).astype(F32).astype(BF16)

    row = lax.broadcasted_iota(jnp.int32, (count, lanes), 0)
    block = lax.broadcasted_iota(jnp.int32, (count, lanes), 1) // tokens
    copy = (row % 2).astype(F32)

    def choose(table, entry, seat, senses):
        base = jnp.zeros((count, lanes), jnp.int32)
        wanted = jnp.zeros((count, lanes), jnp.int32)
        for i, (step, source) in enumerate(table):
            goals = [lax.rem(plane + sense * step + PLANES, PLANES) * SEATS for sense in senses]
            goal = goals[0] if len(goals) == 1 else jnp.where(seat % 2 == 0, goals[0], goals[1])
            base = jnp.where(entry == i, goal, base)
            wanted = jnp.where(entry == i, source, wanted)
        expert = (base + seat).astype(F32)
        hit = jnp.zeros((count, lanes), F32)
        scale = jnp.zeros((count, lanes), F32)
        for k in range(TOPK):
            found = ids[k : k + 1, :] == expert
            hit = jnp.where(found, 1.0, hit)
            scale = jnp.where(found, weights[k : k + 1, :], scale)
        rank = jnp.dot(hit.astype(BF16), before, preferred_element_type=F32)
        chosen = (hit > 0.5) & (jnp.abs(rank - copy) < 0.5) & (block == wanted)
        chosen = jnp.where(chosen, 1.0, 0.0)
        return chosen.astype(BF16), jnp.sum(chosen * scale, axis=1, keepdims=True)

    near, near_weight = choose(NEAR, (row // 2) % 8, row // GROUP, (1, -1))
    far, far_weight = choose(FAR, row // GROUP, (row // 2) % SEATS, (sign,))
    for part in range(parts):
        cut = pl.ds(part * part_width, part_width)
        tile = jnp.concatenate([ref[:, cut] for ref in refs], axis=0)
        rows = jnp.dot(far, tile, preferred_element_type=F32)
        rows = (far_weight * rows).astype(BF16)
        at = 0
        for ref, size in zip(far_refs, CUTS, strict=True):
            ref[:, cut] = rows[at : at + size]
            at += size
        rows = jnp.dot(near, tile, preferred_element_type=F32)
        near_ref[part] = (near_weight * rows).astype(BF16)


def picked(plane, sign, own, behind, ahead, parts):
    width = own.shape[1] - META
    shapes = [(parts, SEATS * GROUP, width // parts)] + [(size, width) for size in CUTS]
    return pl.pallas_call(
        pick_kernel,
        in_specs=[pl.BlockSpec(memory_space=pltpu.SMEM)] + [pl.BlockSpec(memory_space=pltpu.VMEM)] * 3,
        out_shape=[jax.ShapeDtypeStruct(shape, BF16) for shape in shapes],
        compiler_params=SMALL,
    )(jnp.stack([plane, sign]).astype(jnp.int32), own, behind, ahead)


def join_kernel(*refs):
    *in_refs, out_ref = refs
    parts, count, width = out_ref.shape
    to = lax.broadcasted_iota(jnp.int32, (count, count), 0)
    at = lax.broadcasted_iota(jnp.int32, (count, count), 1)
    seat, entry, copy = to // GROUP, (to // 2) % 8, to % 2
    move = (at == entry * GROUP + seat * 2 + copy).astype(F32).astype(BF16)
    for part in range(parts):
        cut = pl.ds(part * width, width)
        rows = jnp.concatenate([ref[:, cut] for ref in in_refs], axis=0)
        out_ref[part] = jnp.dot(move, rows, preferred_element_type=F32).astype(BF16)


def join(pieces, parts):
    rows = sum(piece.shape[0] for piece in pieces)
    return pl.pallas_call(
        join_kernel,
        out_shape=jax.ShapeDtypeStruct((parts, rows, pieces[0].shape[1] // parts), BF16),
        compiler_params=SMALL,
    )(*pieces)


def shift(array, step):
    pairs = []
    for z in range(PLANES):
        for core in range(2):
            goal = (z + (step if core == 0 else -step)) % PLANES
            pairs.append((z * 2 + core, goal * 2 + core))
    return lax.ppermute(array, ("z", "core"), pairs)


def gathered(array, axis):
    count = lax.axis_size(axis)
    copies = jnp.broadcast_to(array[None], (count, *array.shape))
    return lax.all_to_all(copies, axis, split_axis=0, concat_axis=0, tiled=True)


def exchanged(array):
    array = array.reshape(-1, GROUP, array.shape[2])
    return lax.all_to_all(array, ("dp", "x", "core"), split_axis=0, concat_axis=0, tiled=True)


def factor_moves(plane, sign, slots):
    moves = []
    for low, high in ((0, 8), (8, 11), (11, 14), (14, 22)):
        span = SLOTS[low:high]
        size = len(span)
        to = np.arange(SEATS * size * 2)
        seat, entry, copy = to // (size * 2), (to // 2) % size, to % 2
        ahead = np.array([0 if s is None else s[0] for s in span])[entry] * (1 - 2 * (seat % 2))
        behind = np.array([0 if s is None else s[1] for s in span])[entry]
        real = np.array([s is not None for s in span])[entry]
        moves.append(np.stack([ahead, behind, seat * 2 + copy, real]))
    ahead, behind, within, real = np.concatenate(moves, axis=1).astype(np.int32)
    slot = (plane + ahead - sign * behind + 2 * PLANES) % PLANES * GROUP + within
    same = slot[:, None] == jnp.arange(slots, dtype=jnp.int32)[None, :]
    return (same & (real[:, None] > 0)).astype(BF16)


def cut_kernel(in_ref, up_ref, down_ref):
    steps = 2
    chunk = in_ref.shape[0] // steps
    for ref, (low, high) in zip((up_ref, down_ref), HALVES, strict=True):
        size = 2 * (high - low)
        count = chunk // GROUP * size
        row = lax.broadcasted_iota(jnp.int32, (count, chunk), 0)
        goal = lax.broadcasted_iota(jnp.int32, (count, chunk), 1)
        source = (row * (65536 // size + 1)) >> 16
        move = (goal == source * GROUP + 2 * low + row - source * size).astype(F32).astype(BF16)
        for step in range(steps):
            rows = jnp.dot(
                move, in_ref[step * chunk : (step + 1) * chunk], preferred_element_type=F32
            )
            ref[step * count : (step + 1) * count] = rows.astype(BF16)


def halves(array):
    count, rows, width = array.shape
    shapes = [
        jax.ShapeDtypeStruct((count * 2 * (high - low), width), array.dtype) for low, high in HALVES
    ]
    return pl.pallas_call(cut_kernel, out_shape=shapes, compiler_params=SMALL)(
        array.reshape(count * rows, width)
    )


def order_kernel(move_ref, reduced_ref, *out_refs):
    for replica in range(reduced_ref.shape[0]):
        rows = jnp.dot(move_ref[...], reduced_ref[replica], preferred_element_type=F32)
        at = 0
        for ref in out_refs:
            ref[replica] = rows[at : at + ref.shape[1]].astype(BF16)
            at += ref.shape[1]


def ordered(moves, reduced):
    replicas, _, rank = reduced.shape
    sizes = [2 * SEATS * count for count in (8, 3, 3, 8)]
    return pl.pallas_call(
        order_kernel,
        out_shape=[jax.ShapeDtypeStruct((replicas, size, rank), BF16) for size in sizes],
        compiler_params=SMALL,
    )(moves, reduced)


def layer(grad_out, expert_ids, route_weights, hidden_act, projection):
    parts = lax.axis_size("dp")
    tokens, width = grad_out.shape
    rank = projection.shape[2]
    plane, core = lax.axis_index("z"), lax.axis_index("core")
    sign = 1 - 2 * core
    own = pl.pallas_call(
        pack_kernel,
        out_shape=jax.ShapeDtypeStruct((tokens, width + META), BF16),
    )(grad_out, expert_ids.T, route_weights.T)
    behind, ahead = shift(own, LEAP), shift(own, -LEAP)

    basis = gathered(projection[0], "dp").reshape(-1, rank)
    moves = factor_moves(plane, sign, hidden_act.shape[2])
    basis, moves = lax.optimization_barrier((basis, moves))
    reduced = jnp.dot(hidden_act[0, 0], basis, preferred_element_type=F32).astype(BF16)
    reduced = gathered(reduced, "dp")

    near, stay, up2, down2, up3 = picked(plane, sign, own, behind, ahead, parts)
    up2, down2, up3 = shift(up2, 2), shift(down2, -2), shift(up3, 3)
    near, reduced = lax.optimization_barrier((near, reduced))
    near = exchanged(near)
    factors = ordered(moves, reduced)
    far = join([stay, up2, down2, up3], parts)
    far = exchanged(far)
    up1, down1 = halves(near)
    up1, down1 = shift(up1, 1), shift(down1, -1)
    shares = []
    for piece, factor in zip((near, up1, down1, far), factors, strict=True):
        share = lax.dot_general(
            piece.reshape(-1, piece.shape[-1]),
            factor.reshape(-1, rank),
            (((0,), (0,)), ((), ())),
            preferred_element_type=F32,
        )
        shares.append(share)
    early = lax.optimization_barrier(shares[0] + shares[1] + shares[2])
    total = shares[3] + early
    return total.astype(BF16)[None]


def solution(mesh):
    names = ("dp", "z", "x", "core")
    fine = Mesh(mesh.devices.reshape(mesh.shape["dp"], PLANES, -1, 2), names)
    devices = ("z", "x", "core")
    in_specs = (
        P(names, None),
        P(names, None),
        P(names, None),
        P("dp", devices, None, None),
        P(devices, "dp", None),
    )
    out_specs = P(devices, "dp", None)
    return jax.shard_map(layer, mesh=fine, in_specs=in_specs, out_specs=out_specs, check_vma=False)
```
